128 devices in a mesh: rows: 32 (over x, y, core), eig: 4 (over z).
Axes of the slice: x: 4, y: 4, z: 4, core: 2. Of those that a mesh axis runs over, the one named last changes fastest.
Arguments:
- phi_obs: bfloat16 [16384, 4096], P('rows', 'eig'), may hold values from -0.09375 to 0.09375
- counts: int32 [32], P('rows'), may hold values from 1 to 512, as said below
- targets: bfloat16 [16384, 128], P('rows', 'eig'), may hold values from -6 to 6
- spectrum: float32 [4096], replicated, may hold values from 0.1 to 10
- coef_noise: float32 [4096, 128], replicated, may hold values from -6 to 6
- phi_slab: bfloat16 [65536, 4096], P('rows', 'eig'), may hold values from -0.09375 to 0.09375
Outputs:
- factor: float32 [4096, 4096], P('rows', 'eig')
- solved: float32 [4096, 128], P('rows', 'eig')
- slab_prior: float32 [65536, 128], P(('rows', 'eig'))
The draws below stay inside these ranges and needn't reach their ends.
Inputs may be any that keep to these rules, and one draw needn't show every extreme that they name: counts[r] is the number of live rows of shard r, which come first in the shard; some shard is full (512).
All inputs are finite; a program needn't handle non-finite values.
Results may differ from the reference program's by a relative error of at most 0.0029.
Values may be sent and summed in bfloat16 or wider, within the bound.
No kernel may reach another device: no remote copies, remote signals or barrier semaphores. Data moves between devices by JAX's collectives and lax.ppermute only.
A program may use at most 192 MiB of HBM per device.

```python
import math
import jax
import jax.numpy as jnp
from jax import lax

M = 4096
PANEL = 512
SAMPLES = 128
OBS_DEV = 512
SHARDS = 32
OBS = 16384
SLAB = 65536
N_ROWS = 32


def draw_counts(key, part):
    first_key, second_key, third_key = jax.random.split(key, 3)
    first = jax.random.randint(first_key, (SHARDS,), 1, OBS_DEV + 1)
    second = jax.random.randint(second_key, (SHARDS,), 1, OBS_DEV + 1)
    base = jnp.maximum(1, first * second // OBS_DEV)
    chosen = jax.random.randint(third_key, (), 0, SHARDS)
    return jnp.where(jnp.arange(SHARDS) == chosen, OBS_DEV, base).astype(jnp.int32)


def shard_levels(own_key, dims, pieces, low, top_value):
    factor_of = 1.0
    for axis_at, parts in pieces:
        draws = jax.random.uniform(jax.random.fold_in(jax.random.fold_in(own_key, 6), axis_at), (parts,), jnp.float32, low / len(pieces), top_value / len(pieces))
        factor_of = factor_of * jnp.repeat(jnp.exp(draws), dims[axis_at] // parts).reshape((-1,) + (1,) * (len(dims) - 1 - axis_at))
    return factor_of


def scatter_about(key, shape, scale, bound, pieces=(), held_as=jnp.bfloat16):
    values = scale * jax.random.normal(key, shape, jnp.float32)
    if pieces:
        values = values * shard_levels(key, shape, pieces, -0.22, 0.18)
    return jnp.clip(values, -bound, bound).astype(held_as)


def setup_inputs(seed: int = 0) -> dict:
    seeds = jax.random.split(jax.random.key(seed), 7)
    phi_obs = scatter_about(seeds[0], (OBS, M), (OBS_DEV * N_ROWS // 4) ** -0.5, 0.09375, ((0, 32), (1, 4)))
    counts = draw_counts(jax.random.fold_in(seeds[6], 71), 0)
    targets = scatter_about(seeds[2], (OBS, SAMPLES), 1.0, 6.0, ((0, 32), (1, 4)))
    spectrum = jnp.clip(jnp.exp(jax.random.uniform(seeds[3], (M,), jnp.float32, math.log(0.1), math.log(10.0))), 0.1, 10.0)
    coef_noise = scatter_about(seeds[4], (M, SAMPLES), 1.0, 6.0, (), jnp.float32)
    phi_slab = scatter_about(seeds[5], (SLAB, M), M ** -0.5, 0.09375, ((0, 32), (1, 4)))
    return dict(phi_obs=phi_obs, counts=counts, targets=targets, spectrum=spectrum, coef_noise=coef_noise, phi_slab=phi_slab)


def reference(phi_obs, counts, targets, spectrum, coef_noise, phi_slab):
    shards = counts.shape[0]
    rows_each = phi_obs.shape[0] // shards
    position = jnp.arange(rows_each, dtype=jnp.int32)
    keep = (position[None, :] < counts[:, None]).reshape(-1)
    live = jnp.where(keep[:, None], phi_obs, jnp.zeros_like(phi_obs))
    live_targets = jnp.where(keep[:, None], targets, jnp.zeros_like(targets))
    gram = jnp.dot(live.T.astype(jnp.float32), live.astype(jnp.float32), preferred_element_type=jnp.float32)
    order = gram.shape[0]
    precision = gram + jnp.diag(1.0 / spectrum)
    head = jnp.linalg.cholesky(precision[:PANEL, :PANEL])
    lower = jax.scipy.linalg.solve_triangular(head, precision[PANEL:, :PANEL].T, lower=True).T
    trailing = precision[PANEL:, PANEL:] - jnp.dot(lower, lower.T, precision=lax.Precision.HIGHEST)
    top = jnp.concatenate([head, jnp.zeros((PANEL, order - PANEL), jnp.float32)], axis=1)
    bottom = jnp.concatenate([lower, trailing], axis=1)
    factor = jnp.concatenate([top, bottom], axis=0)
    rhs = jnp.dot(live.T.astype(jnp.float32), live_targets.astype(jnp.float32), preferred_element_type=jnp.float32)
    rhs = rhs + coef_noise / jnp.sqrt(spectrum)[:, None]
    first = jax.scipy.linalg.solve_triangular(head, rhs[:PANEL], lower=True)
    rest = rhs[PANEL:] - jnp.dot(lower, first, precision=lax.Precision.HIGHEST)
    solved = jnp.concatenate([first, rest], axis=0)
    scaled = (jnp.sqrt(spectrum)[:, None] * coef_noise).astype(jnp.bfloat16)
    slab_prior = jnp.dot(phi_slab.astype(jnp.float32), scaled.astype(jnp.float32), preferred_element_type=jnp.float32)
    return (factor, solved, slab_prior)
```

```python
import jax
import jax.numpy as jnp
from jax import lax
from jax.sharding import PartitionSpec as P

PANEL = 512
F32 = jnp.float32
BF16 = jnp.bfloat16
HI = lax.Precision.HIGHEST


def rows_perm(move):
    pairs = []
    for i in range(32):
        x, y, c = move(i // 8, (i // 2) % 4, i % 2)
        pairs.append((i, x * 8 + y * 2 + c))
    return pairs


CORE = ("rows", rows_perm(lambda x, y, c: (x, y, 1 - c)))
X_A = ("rows", rows_perm(lambda x, y, c: (x ^ 1, y, c)))
X_B = ("rows", rows_perm(lambda x, y, c: (3 - x, y, c)))
Y_A = ("rows", rows_perm(lambda x, y, c: (x, y ^ 1, c)))
Y_B = ("rows", rows_perm(lambda x, y, c: (x, 3 - y, c)))
Z_A = ("eig", [(i, i ^ 1) for i in range(4)])
Z_B = ("eig", [(i, 3 - i) for i in range(4)])
Z_UP = ("eig", [(i, (i + 1) % 4) for i in range(4)])
Z_DOWN = ("eig", [(i, (i - 1) % 4) for i in range(4)])
Z_FAR = ("eig", [(i, (i + 2) % 4) for i in range(4)])


def move(array, way):
    return lax.ppermute(array, way[0], way[1])


def pick(array, axis, items):
    parts = [lax.index_in_dim(array, i, axis, keepdims=True) for i in items]
    return parts[0] if len(parts) == 1 else lax.concatenate(parts, axis)


def halves(array, axis, low, high, bit):
    a, b = pick(array, axis, low), pick(array, axis, high)
    return jnp.where(bit, b, a), jnp.where(bit, a, b)


class Ring:
    def __init__(self, place, first, second, a_first):
        self.first, self.second = (first, second) if a_first else (second, first)
        if a_first:
            self.low, self.high = (0, 3), (1, 2)
            self.bit1 = (place == 1) | (place == 2)
            self.bit2 = place >= 2
        else:
            self.low, self.high = (0, 1), (2, 3)
            self.bit1 = place >= 2
            self.bit2 = (place & 1) == 1

    def scatter(self, array, axis, types):
        keep, send = halves(array, axis, self.low, self.high, self.bit1)
        got = move(send.astype(types[0]), self.first)
        array = keep.astype(F32) + got.astype(F32)
        keep, send = halves(array, axis, (0,), (1,), self.bit2)
        got = move(send.astype(types[1]), self.second)
        return keep + got.astype(F32)

    def gather(self, array, axis):
        got = move(array, self.second)
        pair = jnp.where(
            self.bit2,
            lax.concatenate([got, array], axis),
            lax.concatenate([array, got], axis),
        )
        got = move(pair, self.first)
        low = jnp.where(self.bit1, got, pair)
        high = jnp.where(self.bit1, pair, got)
        order = self.low + self.high
        both = lax.concatenate([low, high], axis)
        return pick(both, axis, [order.index(i) for i in range(4)])

    def add(self, array):
        array = array + move(array, self.first)
        return array + move(array, self.second)


def on_device(phi_obs, counts, targets, spectrum, coef_noise, phi_slab):
    row = lax.axis_index("rows")
    e = lax.axis_index("eig")
    x, y, c = row // 8, (row // 2) % 4, row % 2
    rings = [
        (Ring(x, X_A, X_B, True), Ring(y, Y_A, Y_B, True), 0),
        (Ring(x, X_A, X_B, False), Ring(y, Y_A, Y_B, False), 0),
        (Ring(y, Y_A, Y_B, True), Ring(x, X_A, X_B, True), 1),
        (Ring(y, Y_A, Y_B, False), Ring(x, X_A, X_B, False), 1),
    ]
    keep = jnp.arange(512, dtype=jnp.int32)[:, None] < counts[0]
    live = jnp.where(keep, phi_obs, jnp.zeros_like(phi_obs))
    live_t = jnp.where(keep, targets, jnp.zeros_like(targets))

    with jax.named_scope("pair_rows"):
        right = jnp.concatenate([live, move(live, CORE)], axis=0)
        tt = jnp.concatenate([live_t, move(live_t, CORE)], axis=0)
        view = right.reshape(1024, 4, 2, 128)
        own = jnp.where(c == 0, view[:, :, 0], view[:, :, 1]).reshape(1024, 512)
    with jax.named_scope("eig_gather"):
        before = move(own, Z_UP)
        after = move(own, Z_DOWN)
        far_a = move(before[:512], Z_UP)
        far_b = move(after[512:], Z_DOWN)
        left = jnp.zeros((4, 1024, 512), BF16)
        left = lax.dynamic_update_slice(left, own[None], (e, 0, 0))
        left = lax.dynamic_update_slice(left, before[None], ((e + 3) % 4, 0, 0))
        left = lax.dynamic_update_slice(left, after[None], ((e + 1) % 4, 0, 0))
        left = lax.dynamic_update_slice(left, far_a[None], ((e + 2) % 4, 0, 0))
        left = lax.dynamic_update_slice(left, far_b[None], ((e + 2) % 4, 512, 0))

    with jax.named_scope("slab"):
        spectrum_block = lax.dynamic_slice_in_dim(spectrum, e * 1024, 1024, 0)
        noise_block = lax.dynamic_slice_in_dim(coef_noise, e * 1024, 1024, 0)
        scaled = (jnp.sqrt(spectrum_block)[:, None] * noise_block).astype(BF16)
        slab = jnp.dot(phi_slab, scaled, preferred_element_type=F32).reshape(4, 2, 256, 128)
        slab_prior = jnp.concatenate(
            [
                Ring(e, Z_A, Z_B, True).scatter(slab[:, 0], 0, (BF16, F32)),
                Ring(e, Z_A, Z_B, False).scatter(slab[:, 1], 0, (BF16, F32)),
            ],
            axis=1,
        ).reshape(512, 128)

    with jax.named_scope("panel"):
        pcols = left[0, :, :256]
        got = move(pcols, CORE)
        pother = jnp.concatenate([got[512:], got[:512]], axis=0)
        even = jnp.where(c == 0, pcols, pother).reshape(1024, 2, 1, 128)
        odd = jnp.where(c == 0, pother, pcols).reshape(1024, 2, 1, 128)
        pall = jnp.concatenate([even, odd], axis=2).reshape(1024, 512)
        contract0 = (((0,), (0,)), ((), ()))
        part = lax.dot_general(
            pcols, jnp.concatenate([right, pall], axis=1), contract0, preferred_element_type=F32
        )
        rhs_part = lax.dot_general(
            tt, left, (((0,), (1,)), ((), ())), preferred_element_type=F32
        ).reshape(256, 256)
        part = jnp.concatenate([part, rhs_part], axis=1).reshape(4, 4, 16, 1792)
        sums = []
        for s, (one, two, _) in enumerate(rings):
            piece = one.scatter(part[s], 0, (F32, F32))
            piece = two.add(piece)
            sums.append(one.gather(piece, 0))
        mine = jnp.stack(sums).reshape(256, 1792)
        other = move(mine, CORE)
        even, odd = jnp.where(c == 0, mine, other), jnp.where(c == 0, other, mine)
        panel = jnp.stack(
            [even[:, :1536].reshape(2, 128, 1536), odd[:, :1536].reshape(2, 128, 1536)], axis=1
        ).reshape(512, 1536)
        rhs_t = jnp.stack(
            [even[:, 1536:].reshape(32, 16, 128), odd[:, 1536:].reshape(32, 16, 128)], axis=2
        ).reshape(32, 4096)
        inv_prior = 1.0 / spectrum
        k_ids = jnp.arange(PANEL, dtype=jnp.int32)
        col_ids = e * 1024 + jnp.arange(1024, dtype=jnp.int32)
        p11 = panel[:, 1024:] + jnp.where(
            k_ids[:, None] == k_ids[None, :], inv_prior[:PANEL][:, None], 0.0
        )
        t_e = panel[:, :1024] + jnp.where(
            k_ids[:, None] == col_ids[None, :], inv_prior[:PANEL][:, None], 0.0
        )
        piece = lax.dynamic_slice_in_dim(t_e, (row % 8) * 128, 128, 1)
        up, down, far = move(piece, Z_UP), move(piece, Z_DOWN), move(piece, Z_FAR)
        shift = (x - e) % 4
        t_r = jnp.where(
            shift == 0, piece, jnp.where(shift == 1, down, jnp.where(shift == 2, far, up))
        )

    with jax.named_scope("gram"):
        blocks = []
        for s, (one, two, axis) in enumerate(rings):
            g = lax.dot_general(
                left,
                right[:, 256 * s : 256 * s + 256],
                (((1,), (0,)), ((), ())),
                preferred_element_type=F32,
            ).astype(BF16).reshape(4, 4, 128, 256)
            g = one.scatter(g, axis, (BF16, BF16))
            g = two.scatter(g, 1 - axis, (F32, F32))
            blocks.append(g.reshape(128, 256))
        gram = jnp.concatenate(blocks, axis=1)

    with jax.named_scope("rhs"):
        noise_cols = lax.dynamic_slice_in_dim(coef_noise, e * 32, 32, 1)
        rhs = rhs_t.T + noise_cols / jnp.sqrt(spectrum)[:, None]

    with jax.named_scope("head"):
        head = jnp.linalg.cholesky(p11)
        winv = jax.scipy.linalg.solve_triangular(head, jnp.eye(PANEL, dtype=F32), lower=True)

    with jax.named_scope("solve"):
        l_e = jnp.dot(winv, t_e, precision=HI)
        l_r = jnp.dot(winv, t_r, precision=HI)
        first = jnp.dot(winv, rhs[:PANEL], precision=HI)
        row_ids = row * 128 + jnp.arange(128, dtype=jnp.int32)
        top = row * 128 < PANEL
        head_rows = lax.dynamic_slice_in_dim(head, jnp.minimum(row, 3) * 128, 128, 0)
        my_rows = jnp.where(top, head_rows, l_r.T)
        inv_rows = lax.dynamic_slice_in_dim(inv_prior, row * 128, 128, 0)
        block = gram + jnp.where(row_ids[:, None] == col_ids[None, :], inv_rows[:, None], 0.0)
        schur = block - lax.dot_general(
            l_r, l_e, (((0,), (0,)), ((), ())), precision=HI, preferred_element_type=F32
        )
        right_part = jnp.where(top, 0.0, schur)
        factor = jnp.where(
            col_ids[None, :] < PANEL, jnp.pad(my_rows, ((0, 0), (0, 512))), right_part
        )
        my_rhs = lax.dynamic_slice_in_dim(rhs, row * 128, 128, 0)
        first_rows = lax.dynamic_slice_in_dim(first, jnp.minimum(row, 3) * 128, 128, 0)
        solved = jnp.where(
            top,
            first_rows,
            my_rhs
            - lax.dot_general(
                l_r, first, (((0,), (0,)), ((), ())), precision=HI, preferred_element_type=F32
            ),
        )
    return (factor, solved, slab_prior)


def solution(mesh):
    return jax.shard_map(
        on_device,
        mesh=mesh,
        in_specs=(P("rows", "eig"), P("rows"), P("rows", "eig"), P(), P(), P("rows", "eig")),
        out_specs=(P("rows", "eig"), P("rows", "eig"), P(("rows", "eig"), None)),
        check_vma=False,
    )
```

```python
import jax
import jax.numpy as jnp
from jax import lax
from jax.experimental import pallas as pl
from jax.experimental.pallas import tpu as pltpu
from jax.sharding import PartitionSpec as P

PANEL = 512
F32 = jnp.float32
BF16 = jnp.bfloat16
HI = lax.Precision.HIGHEST


def rows_perm(move):
    pairs = []
    for i in range(32):
        x, y, c = move(i // 8, (i // 2) % 4, i % 2)
        pairs.append((i, x * 8 + y * 2 + c))
    return pairs


CORE = ("rows", rows_perm(lambda x, y, c: (x, y, 1 - c)))
X_A = ("rows", rows_perm(lambda x, y, c: (x ^ 1, y, c)))
X_B = ("rows", rows_perm(lambda x, y, c: (3 - x, y, c)))
Y_A = ("rows", rows_perm(lambda x, y, c: (x, y ^ 1, c)))
Y_B = ("rows", rows_perm(lambda x, y, c: (x, 3 - y, c)))
Z_A = ("eig", [(i, i ^ 1) for i in range(4)])
Z_B = ("eig", [(i, 3 - i) for i in range(4)])
Z_UP = ("eig", [(i, (i + 1) % 4) for i in range(4)])
Z_DOWN = ("eig", [(i, (i - 1) % 4) for i in range(4)])
Z_FAR = ("eig", [(i, (i + 2) % 4) for i in range(4)])


def move(array, way):
    return lax.ppermute(array, way[0], way[1])


def pick(array, axis, items):
    parts = [lax.index_in_dim(array, i, axis, keepdims=True) for i in items]
    return parts[0] if len(parts) == 1 else lax.concatenate(parts, axis)


def halves(array, axis, low, high, bit):
    a, b = pick(array, axis, low), pick(array, axis, high)
    return jnp.where(bit, b, a), jnp.where(bit, a, b)


class Ring:
    def __init__(self, place, first, second, a_first):
        self.first, self.second = (first, second) if a_first else (second, first)
        if a_first:
            self.low, self.high = (0, 3), (1, 2)
            self.bit1 = (place == 1) | (place == 2)
            self.bit2 = place >= 2
        else:
            self.low, self.high = (0, 1), (2, 3)
            self.bit1 = place >= 2
            self.bit2 = (place & 1) == 1

    def scatter(self, array, axis, types):
        keep, send = halves(array, axis, self.low, self.high, self.bit1)
        got = move(send.astype(types[0]), self.first)
        array = keep.astype(F32) + got.astype(F32)
        keep, send = halves(array, axis, (0,), (1,), self.bit2)
        got = move(send.astype(types[1]), self.second)
        return keep + got.astype(F32)

    def gather(self, array, axis):
        got = move(array, self.second)
        pair = jnp.where(
            self.bit2,
            lax.concatenate([got, array], axis),
            lax.concatenate([array, got], axis),
        )
        got = move(pair, self.first)
        low = jnp.where(self.bit1, got, pair)
        high = jnp.where(self.bit1, pair, got)
        order = self.low + self.high
        both = lax.concatenate([low, high], axis)
        return pick(both, axis, [order.index(i) for i in range(4)])

    def add(self, array):
        array = array + move(array, self.first)
        return array + move(array, self.second)


def head_kernel(p_ref, u_ref, w_ref, a_ref):
    a_ref[...] = p_ref[...]
    u_ref[...] = jnp.zeros_like(u_ref)
    w_ref[...] = jnp.zeros_like(w_ref)
    sub = lax.broadcasted_iota(jnp.int32, (8, 128), 0)
    lane = lax.broadcasted_iota(jnp.int32, (8, 128), 1)

    def block(b, carry):
        at = pl.multiple_of(b * 128, 128)
        d, n = [], []
        for t in range(16):
            d.append(a_ref[pl.ds(at + 8 * t, 8), pl.ds(at, 128)])
            n.append(jnp.where(lane == sub + 8 * t, 1.0, 0.0).astype(F32))
        for j in range(127):
            t0, s = j // 8, j % 8
            inv = 1.0 / d[t0][s : s + 1, j : j + 1]
            row_d = d[t0][s : s + 1, :] * inv
            row_n = n[t0][s : s + 1, :] * inv
            for t in range(t0 if s < 7 else t0 + 1, 16):
                m = jnp.broadcast_to(d[t][:, j : j + 1], (8, 128))
                if t == t0:
                    m = jnp.where(sub > s, m, 0.0)
                d[t] = d[t] - m * row_d
                n[t] = n[t] - m * row_n
        us, ws = [], []
        for t in range(16):
            diag = jnp.sum(jnp.where(lane == sub + 8 * t, d[t], 0.0), axis=1, keepdims=True)
            r = 1.0 / jnp.sqrt(diag)
            us.append(jnp.where(lane >= sub + 8 * t, d[t] * r, 0.0))
            ws.append(n[t] * r)
        u, w = jnp.concatenate(us, axis=0), jnp.concatenate(ws, axis=0)
        strip = jnp.dot(w, a_ref[pl.ds(at, 128), :], precision=HI, preferred_element_type=F32)
        cols = lax.broadcasted_iota(jnp.int32, (128, 512), 1)
        strip = jnp.where(cols >= at + 128, strip, 0.0)
        u_ref[pl.ds(at, 128), :] = strip
        u_ref[pl.ds(at, 128), pl.ds(at, 128)] = u
        mine = lax.dot_general(
            u_ref[:, pl.ds(at, 128)], w_ref[...], (((0,), (0,)), ((), ())),
            precision=HI, preferred_element_type=F32,
        )
        w_ref[pl.ds(at, 128), :] = -jnp.dot(w, mine, precision=HI, preferred_element_type=F32)
        w_ref[pl.ds(at, 128), pl.ds(at, 128)] = w
        a_ref[...] = a_ref[...] - lax.dot_general(
            strip, strip, (((0,), (0,)), ((), ())), precision=HI, preferred_element_type=F32
        )
        return carry

    lax.fori_loop(0, 4, block, 0)


def head_factor(p11, interpret=False):
    shape = jax.ShapeDtypeStruct((PANEL, PANEL), F32)
    return pl.pallas_call(
        head_kernel,
        out_shape=(shape, shape),
        scratch_shapes=[pltpu.VMEM((PANEL, PANEL), F32)],
        interpret=interpret,
        name="head_factor",
    )(p11)


def on_device(phi_obs, counts, targets, spectrum, coef_noise, phi_slab):
    row = lax.axis_index("rows")
    e = lax.axis_index("eig")
    x, y, c = row // 8, (row // 2) % 4, row % 2
    rings = [
        (Ring(x, X_A, X_B, True), Ring(y, Y_A, Y_B, True), 0),
        (Ring(x, X_A, X_B, False), Ring(y, Y_A, Y_B, False), 0),
        (Ring(y, Y_A, Y_B, True), Ring(x, X_A, X_B, True), 1),
        (Ring(y, Y_A, Y_B, False), Ring(x, X_A, X_B, False), 1),
    ]
    keep = jnp.arange(512, dtype=jnp.int32)[:, None] < counts[0]
    live = jnp.where(keep, phi_obs, jnp.zeros_like(phi_obs))
    live_t = jnp.where(keep, targets, jnp.zeros_like(targets))

    with jax.named_scope("pair_rows"):
        right = jnp.concatenate([live, move(live, CORE)], axis=0)
        tt = jnp.concatenate([live_t, move(live_t, CORE)], axis=0)
        view = right.reshape(1024, 4, 2, 128)
        own = jnp.where(c == 0, view[:, :, 0], view[:, :, 1]).reshape(1024, 512)
    with jax.named_scope("eig_gather"):
        before = move(own, Z_UP)
        after = move(own, Z_DOWN)
        far_a = move(before[:512], Z_UP)
        far_b = move(after[512:], Z_DOWN)
        left = jnp.zeros((4, 1024, 512), BF16)
        left = lax.dynamic_update_slice(left, own[None], (e, 0, 0))
        left = lax.dynamic_update_slice(left, before[None], ((e + 3) % 4, 0, 0))
        left = lax.dynamic_update_slice(left, after[None], ((e + 1) % 4, 0, 0))
        left = lax.dynamic_update_slice(left, far_a[None], ((e + 2) % 4, 0, 0))
        left = lax.dynamic_update_slice(left, far_b[None], ((e + 2) % 4, 512, 0))

    with jax.named_scope("slab"):
        spectrum_block = lax.dynamic_slice_in_dim(spectrum, e * 1024, 1024, 0)
        noise_block = lax.dynamic_slice_in_dim(coef_noise, e * 1024, 1024, 0)
        scaled = (jnp.sqrt(spectrum_block)[:, None] * noise_block).astype(BF16)
        slab = jnp.dot(phi_slab, scaled, preferred_element_type=F32).reshape(4, 2, 256, 128)
        slab_prior = jnp.concatenate(
            [
                Ring(e, Z_A, Z_B, True).scatter(slab[:, 0], 0, (BF16, F32)),
                Ring(e, Z_A, Z_B, False).scatter(slab[:, 1], 0, (BF16, F32)),
            ],
            axis=1,
        ).reshape(512, 128)

    with jax.named_scope("panel"):
        pcols = left[0, :, :256]
        got = move(pcols, CORE)
        pother = jnp.concatenate([got[512:], got[:512]], axis=0)
        even = jnp.where(c == 0, pcols, pother).reshape(1024, 2, 1, 128)
        odd = jnp.where(c == 0, pother, pcols).reshape(1024, 2, 1, 128)
        pall = jnp.concatenate([even, odd], axis=2).reshape(1024, 512)
        contract0 = (((0,), (0,)), ((), ()))
        part = lax.dot_general(
            pcols, jnp.concatenate([right, pall], axis=1), contract0, preferred_element_type=F32
        )
        rhs_part = lax.dot_general(
            tt, left, (((0,), (1,)), ((), ())), preferred_element_type=F32
        ).reshape(256, 256)
        part = jnp.concatenate([part, rhs_part], axis=1).reshape(4, 4, 16, 1792)
        sums = []
        for s, (one, two, _) in enumerate(rings):
            piece = one.scatter(part[s], 0, (F32, F32))
            piece = two.add(piece)
            sums.append(one.gather(piece, 0))
        mine = jnp.stack(sums).reshape(256, 1792)
        other = move(mine, CORE)
        even, odd = jnp.where(c == 0, mine, other), jnp.where(c == 0, other, mine)
        panel = jnp.stack(
            [even[:, :1536].reshape(2, 128, 1536), odd[:, :1536].reshape(2, 128, 1536)], axis=1
        ).reshape(512, 1536)
        rhs_t = jnp.stack(
            [even[:, 1536:].reshape(32, 16, 128), odd[:, 1536:].reshape(32, 16, 128)], axis=2
        ).reshape(32, 4096)
        inv_prior = 1.0 / spectrum
        k_ids = jnp.arange(PANEL, dtype=jnp.int32)
        col_ids = e * 1024 + jnp.arange(1024, dtype=jnp.int32)
        p11 = panel[:, 1024:] + jnp.where(
            k_ids[:, None] == k_ids[None, :], inv_prior[:PANEL][:, None], 0.0
        )
        t_e = panel[:, :1024] + jnp.where(
            k_ids[:, None] == col_ids[None, :], inv_prior[:PANEL][:, None], 0.0
        )
        piece = lax.dynamic_slice_in_dim(t_e, (row % 8) * 128, 128, 1)
        up, down, far = move(piece, Z_UP), move(piece, Z_DOWN), move(piece, Z_FAR)
        shift = (x - e) % 4
        t_r = jnp.where(
            shift == 0, piece, jnp.where(shift == 1, down, jnp.where(shift == 2, far, up))
        )

    with jax.named_scope("gram"):
        blocks = []
        for s, (one, two, axis) in enumerate(rings):
            g = lax.dot_general(
                left,
                right[:, 256 * s : 256 * s + 256],
                (((1,), (0,)), ((), ())),
                preferred_element_type=F32,
            ).astype(BF16).reshape(4, 4, 128, 256)
            g = one.scatter(g, axis, (BF16, BF16))
            g = two.scatter(g, 1 - axis, (F32, F32))
            blocks.append(g.reshape(128, 256))
        gram = jnp.concatenate(blocks, axis=1)

    with jax.named_scope("rhs"):
        noise_cols = lax.dynamic_slice_in_dim(coef_noise, e * 32, 32, 1)
        rhs = rhs_t.T + noise_cols / jnp.sqrt(spectrum)[:, None]

    with jax.named_scope("head"):
        upper, winv = head_factor(p11)

    with jax.named_scope("solve"):
        l_e = jnp.dot(winv, t_e, precision=HI)
        l_r = jnp.dot(winv, t_r, precision=HI)
        first = jnp.dot(winv, rhs[:PANEL], precision=HI)
        row_ids = row * 128 + jnp.arange(128, dtype=jnp.int32)
        top = row * 128 < PANEL
        head_cols = lax.dynamic_slice_in_dim(upper, jnp.minimum(row, 3) * 128, 128, 1)
        my_rows = jnp.where(top, head_cols, l_r).T
        inv_rows = lax.dynamic_slice_in_dim(inv_prior, row * 128, 128, 0)
        block = gram + jnp.where(row_ids[:, None] == col_ids[None, :], inv_rows[:, None], 0.0)
        schur = block - lax.dot_general(
            l_r, l_e, (((0,), (0,)), ((), ())), precision=HI, preferred_element_type=F32
        )
        right_part = jnp.where(top, 0.0, schur)
        factor = jnp.where(
            col_ids[None, :] < PANEL, jnp.pad(my_rows, ((0, 0), (0, 512))), right_part
        )
        my_rhs = lax.dynamic_slice_in_dim(rhs, row * 128, 128, 0)
        first_rows = lax.dynamic_slice_in_dim(first, jnp.minimum(row, 3) * 128, 128, 0)
        solved = jnp.where(
            top,
            first_rows,
            my_rhs
            - lax.dot_general(
                l_r, first, (((0,), (0,)), ((), ())), precision=HI, preferred_element_type=F32
            ),
        )
    return (factor, solved, slab_prior)


def solution(mesh):
    return jax.shard_map(
        on_device,
        mesh=mesh,
        in_specs=(P("rows", "eig"), P("rows"), P("rows", "eig"), P(), P(), P("rows", "eig")),
        out_specs=(P("rows", "eig"), P("rows", "eig"), P(("rows", "eig"), None)),
        check_vma=False,
    )
```
